32 devices in a mesh: ctx: 8 (over z, y), head: 4 (over x, core).
Axes of the slice: x: 2, y: 2, z: 4, core: 2. Of those that a mesh axis runs over, the one named last changes fastest.
Arguments:
- queries: bfloat16 [4096, 4, 512], P('ctx', 'head'), may hold values from -5 to 5
- keys: bfloat16 [4096, 512], P('ctx'), may hold values from -5 to 5
- values: bfloat16 [4096, 512], P('ctx'), may hold values from -5 to 5
- grad_out: bfloat16 [4096, 4, 512], P('ctx', 'head'), may hold values from -24 to 24
- doc_lengths: int32 [8], replicated, may hold values from 1 to 1024, 4096 in all
Outputs:
- query_grad: bfloat16 [4096, 4, 512], P('ctx', 'head')
- key_grad: bfloat16 [4096, 512], P(('ctx', 'head'))
- value_grad: bfloat16 [4096, 512], P(('ctx', 'head'))
The draws below stay inside these ranges and needn't reach their ends.
Inputs may be any that keep to these rules, and one draw needn't show every extreme that they name: `doc_lengths`: documents packed one after another; the lengths sum to 4096 and the longest has exactly 1024 tokens.
All inputs are finite; a program needn't handle non-finite values.
Results may differ from the reference program's by a relative error of at most 0.011.
Values may be sent and summed in bfloat16 or wider, within the bound.
No kernel may reach another device: no remote copies, remote signals or barrier semaphores. Data moves between devices by JAX's collectives and lax.ppermute only.
A program may use at most 64 MiB of HBM per device.

```python
import math
import jax
import jax.numpy as jnp
import numpy as np
from jax import lax

HD = 128
GROUP = 4
KVH = 4
TOK_DEV = 512
HOPS = 2
SEQ = 4096
DOC_MAX = 1024
NDOCS = 8


def draw_queries(key, part):
    shape = (SEQ, GROUP, KVH * HD)
    base = jnp.clip(jax.random.normal(jax.random.fold_in(key, 1), shape, jnp.float32), -4.5, 4.5)
    return base.astype(jnp.bfloat16)


def draw_keys(key, part):
    shape = (SEQ, KVH * HD)
    base = jnp.clip(jax.random.normal(jax.random.fold_in(key, 2), shape, jnp.float32), -4.5, 4.5)
    return base.astype(jnp.bfloat16)


def steps_of(rng, shape, split, smallest, top_value):
    factor_of, own = 1.0, jax.random.fold_in(rng, 6)
    for dim, shards_of in split:
        draws = jnp.exp(jax.random.uniform(jax.random.fold_in(own, dim), (shards_of,), jnp.float32, smallest / len(split), top_value / len(split)))
        factor_of = factor_of * jnp.repeat(draws, shape[dim] // shards_of).reshape([-1 if axis == dim else 1 for axis in range(len(shape))])
    return factor_of


def profile(number_of, total, reach, skew):
    weights = [(1 << 20) // math.isqrt(standing ** skew) + 1 for standing in range(2, number_of + 1)]
    surplus, given = total - reach - (number_of - 1), [1] * (number_of - 1)
    while surplus > 0:
        movable = [i for i in range(number_of - 1) if given[i] < reach]
        pool, budget = sum([weights[i] for i in movable]), surplus
        for i in movable:
            extra = min(reach - given[i], max(1, budget * weights[i] // pool), surplus)
            given[i] = given[i] + extra
            surplus = surplus - extra
    return np.array([reach] + given)


def uneven(key, count, total, bound, slope):
    if count == 2:
        one = jax.random.randint(key, (), max(1, total - bound), min(bound, total - 1) + 1)
        return jnp.stack([one, total - one])
    tallies = jnp.asarray(profile(count, total, bound, slope), jnp.int32)
    twos = (count - 1) // 2
    giver, taker = tallies[1:1 + 2 * twos:2], tallies[2:2 + 2 * twos:2]
    room = jnp.minimum(giver - 1, bound - taker)
    shifted = jax.random.randint(jax.random.fold_in(key, 1), (twos,), 0, 1 << 20) % (room + 1)
    tallies = tallies.at[1:1 + 2 * twos:2].set(giver - shifted).at[2:2 + 2 * twos:2].set(taker + shifted)
    return tallies[jax.random.permutation(jax.random.fold_in(key, 2), count)]


def bell_draw(stream_key, dims, spread, reach, cuts=(), kind=jnp.bfloat16):
    result = spread * jax.random.normal(stream_key, dims, jnp.float32)
    if cuts:
        result = result * steps_of(stream_key, dims, cuts, -0.22, 0.18)
    return jnp.clip(result, -reach, reach).astype(kind)


def setup_inputs(seed: int = 0) -> dict:
    key_list = jax.random.split(jax.random.key(seed), 6)
    return {
        "queries": draw_queries(jax.random.fold_in(key_list[5], 71), 0),
        "keys": draw_keys(jax.random.fold_in(key_list[5], 71), 0),
        "values": bell_draw(key_list[2], (SEQ, KVH * HD), 1.0, 5.0, ((0, 8),)),
        "grad_out": bell_draw(key_list[3], (SEQ, GROUP, KVH * HD), 4.0, 24.0, ((0, 8), (1, 4))),
        "doc_lengths": uneven(key_list[4], NDOCS, SEQ, DOC_MAX, 2).astype(jnp.int32),
    }


def doc_index(doc_lengths, positions):
    doc_ends = jnp.cumsum(doc_lengths).astype(jnp.int32)
    return lax.optimization_barrier(jnp.sum((doc_ends[None, :] <= positions[:, None]).astype(jnp.int32), axis=1)).astype(jnp.int32)

def reference(queries, keys, values, grad_out, doc_lengths):
    reach_rows = HOPS * TOK_DEV
    window_rows = reach_rows + TOK_DEV
    score_scale = 1.0 / math.sqrt(HD)
    lead_zeros = jnp.zeros((reach_rows, KVH * HD), keys.dtype)
    padded_keys = jnp.concatenate([lead_zeros, keys], axis=0)
    padded_values = jnp.concatenate([lead_zeros, values], axis=0)
    local_rows = jnp.arange(TOK_DEV, dtype=jnp.int32)
    window_offsets = jnp.arange(window_rows, dtype=jnp.int32)

    def one_block(totals, block_index):
        key_grads, value_grads = totals
        row_start = (block_index * TOK_DEV).astype(jnp.int32)
        q_block = lax.dynamic_slice_in_dim(queries, row_start, TOK_DEV, 0).astype(jnp.float32).reshape(TOK_DEV, GROUP, KVH, HD)
        g_block = lax.dynamic_slice_in_dim(grad_out, row_start, TOK_DEV, 0).astype(jnp.float32).reshape(TOK_DEV, GROUP, KVH, HD)
        k_window = lax.dynamic_slice_in_dim(padded_keys, row_start, window_rows, 0).astype(jnp.float32).reshape(window_rows, KVH, HD)
        v_window = lax.dynamic_slice_in_dim(padded_values, row_start, window_rows, 0).astype(jnp.float32).reshape(window_rows, KVH, HD)
        q_pos = row_start + local_rows
        k_pos = row_start - reach_rows + window_offsets
        same_doc = doc_index(doc_lengths, k_pos)[None, :] == doc_index(doc_lengths, q_pos)[:, None]
        allowed = (k_pos[None, :] <= q_pos[:, None]) & (k_pos[None, :] >= 0) & same_doc
        raw_scores = jnp.einsum('tmgd,ugd->mgtu', q_block, k_window) * score_scale
        raw_scores = jnp.where(allowed[None, None], raw_scores, -jnp.inf)
        row_top = lax.optimization_barrier(jnp.max(raw_scores, axis=-1, keepdims=True))
        log_norm = row_top + jnp.log(lax.optimization_barrier(jnp.sum(jnp.exp(raw_scores - row_top), axis=-1, keepdims=True)))
        weights = jnp.exp(raw_scores - log_norm)
        weights_b = lax.optimization_barrier(weights.astype(jnp.bfloat16)).astype(jnp.float32)
        attn_out = jnp.einsum('mgtu,ugd->tmgd', weights_b, v_window)
        row_delta = jnp.einsum('tmgd,tmgd->mgt', g_block, attn_out)
        weight_grads = jnp.einsum('tmgd,ugd->mgtu', g_block, v_window)
        score_grads = weights * (weight_grads - row_delta[..., None]) * score_scale
        score_grads = lax.optimization_barrier(score_grads.astype(jnp.bfloat16)).astype(jnp.float32)
        query_grads = jnp.einsum('mgtu,ugd->tmgd', score_grads, k_window)
        key_part = jnp.einsum('mgtu,tmgd->ugd', score_grads, q_block).reshape(window_rows, KVH * HD)
        value_part = jnp.einsum('mgtu,tmgd->ugd', weights_b, g_block).reshape(window_rows, KVH * HD)
        key_grads = lax.dynamic_update_slice_in_dim(key_grads, lax.dynamic_slice_in_dim(key_grads, row_start, window_rows, 0) + key_part, row_start, 0)
        value_grads = lax.dynamic_update_slice_in_dim(value_grads, lax.dynamic_slice_in_dim(value_grads, row_start, window_rows, 0) + value_part, row_start, 0)
        return ((key_grads, value_grads), query_grads.reshape(TOK_DEV, GROUP, KVH * HD).astype(jnp.bfloat16))
    empty_grads = jnp.zeros((SEQ + reach_rows, KVH * HD), jnp.float32)
    block_count = SEQ // TOK_DEV
    finals, query_blocks = lax.scan(one_block, (empty_grads, empty_grads), jnp.arange(block_count, dtype=jnp.int32))
    query_grad = query_blocks.reshape(SEQ, GROUP, KVH * HD)
    key_grad = finals[0][reach_rows:].astype(jnp.bfloat16)
    value_grad = finals[1][reach_rows:].astype(jnp.bfloat16)
    return (query_grad, key_grad, value_grad)
```

```python
import functools
import math

import jax
import jax.numpy as jnp
from jax import lax
from jax.experimental import pallas as pl
from jax.experimental.pallas import tpu as pltpu
from jax.sharding import PartitionSpec as P

HD = 128
HOPS = 2
LOG2E = math.log2(math.e)
NEG = -1e30


def shifted(value, axis, steps):
    count = lax.axis_size(axis)
    first, last = (max(0, -steps), min(count, count - steps))
    return lax.ppermute(value, axis, [(source, source + steps) for source in range(first, last)])


def nt(a, b):
    return lax.dot_general(a, b, (((1,), (1,)), ((), ())), preferred_element_type=jnp.float32)


def nn(a, b):
    return lax.dot_general(a, b, (((1,), (0,)), ((), ())), preferred_element_type=jnp.float32)


def attention_body(
    scale, tq, tk, start_ref, q_ref, g_ref, kv2_ref, kv1_ref, kv0_ref, dq_ref, d2_ref, d1_ref, d0_ref,
    bias, s_scr, p_scr, dp_scr, dk_acc, dv_acc, kt_scr,
):
    members, rows, hd = q_ref.shape
    blocks = (kv2_ref, kv1_ref, kv0_ref)
    back = HOPS * rows
    span = back + tq
    nk = span // tk
    c = scale * LOG2E

    def keys_at(which, first):
        return blocks[first // rows][which, first % rows : first % rows + tk, :]

    dk_acc[...] = jnp.zeros_like(dk_acc)
    dv_acc[...] = jnp.zeros_like(dv_acc)
    for index, ref in enumerate(blocks):
        kt_scr[:, index * rows : (index + 1) * rows] = ref[0].T
    for off in range(0, rows, tq):
        start = start_ref[:, off : off + tq]
        for j in range(0, span, tk):
            t = lax.broadcasted_iota(jnp.int32, (tk, tq), 0) + (off - back + j)
            allowed = t >= start
            if j + tk > back:
                allowed &= t <= lax.broadcasted_iota(jnp.int32, (tk, tq), 1) + off
            bias[j : j + tk, :] = jnp.where(allowed, 0.0, NEG)

        def one_head(m, _):
            q = q_ref[m, off : off + tq, :]
            top = jnp.full((8, tq), NEG, jnp.float32)
            for j in range(0, span, tk):
                s = nt(keys_at(0, off + j), q) + bias[j : j + tk, :]
                s_scr[j : j + tk, :] = s
                top = jnp.maximum(top, jnp.max(s.reshape(tk // 8, 8, tq), axis=0))
            top = jnp.max(top, axis=0, keepdims=True)
            total = jnp.zeros((8, tq), jnp.float32)
            for j in range(0, span, tk):
                p = jnp.exp2((s_scr[j : j + tk, :] - top) * c)
                total = total + jnp.sum(p.reshape(tk // 8, 8, tq), axis=0)
                p_scr[j : j + tk, :] = p.astype(jnp.bfloat16)
            inverse = 1.0 / jnp.sum(total, axis=0, keepdims=True)
            gt = (g_ref[m, off : off + tq, :].T.astype(jnp.float32) * inverse).astype(jnp.bfloat16)
            delta = jnp.zeros((8, tq), jnp.float32)
            for j in range(0, span, tk):
                dp = nn(keys_at(1, off + j), gt)
                dp_scr[j : j + tk, :] = dp
                wdp = p_scr[j : j + tk, :].astype(jnp.float32) * dp
                delta = delta + jnp.sum(wdp.reshape(tk // 8, 8, tq), axis=0)
            delta = jnp.sum(delta, axis=0, keepdims=True) * inverse
            dqt = jnp.zeros((hd, tq), jnp.float32)
            for j in range(0, span, tk):
                p = p_scr[j : j + tk, :]
                ds = (p.astype(jnp.float32) * (dp_scr[j : j + tk, :] - delta)).astype(jnp.bfloat16)
                dv_acc[off + j : off + j + tk, :] += nt(p, gt)
                dk_acc[off + j : off + j + tk, :] += nn(ds, q)
                dqt = dqt + nn(kt_scr[:, off + j : off + j + tk], ds)
            dq_ref[m, off : off + tq, :] = (dqt * scale).T.astype(dq_ref.dtype)
            return 0

        lax.fori_loop(0, members, one_head, 0)
    for index, ref in enumerate((d2_ref, d1_ref, d0_ref)):
        part = slice(index * rows, (index + 1) * rows)
        ref[0] = (dk_acc[part, :] * scale).astype(ref.dtype)
        ref[1] = dv_acc[part, :].astype(ref.dtype)


def attention(start, q, g, kv2, kv1, kv0):
    members, rows, hd = q.shape
    tq = tk = min(256, rows)
    span, window = HOPS * rows + tq, (HOPS + 1) * rows
    vmem = pl.BlockSpec(memory_space=pltpu.VMEM)
    return pl.pallas_call(
        functools.partial(attention_body, 1.0 / math.sqrt(hd), tq, tk),
        out_shape=(
            jax.ShapeDtypeStruct(q.shape, jnp.bfloat16),
            jax.ShapeDtypeStruct(kv2.shape, jnp.bfloat16),
            jax.ShapeDtypeStruct(kv2.shape, jnp.bfloat16),
            jax.ShapeDtypeStruct(kv2.shape, jnp.float32),
        ),
        in_specs=[vmem] * 6,
        out_specs=(vmem,) * 4,
        scratch_shapes=[
            pltpu.VMEM((span, tq), jnp.float32),
            pltpu.VMEM((span, tq), jnp.float32),
            pltpu.VMEM((span, tq), jnp.bfloat16),
            pltpu.VMEM((span, tq), jnp.float32),
            pltpu.VMEM((window, hd), jnp.float32),
            pltpu.VMEM((window, hd), jnp.float32),
            pltpu.VMEM((hd, window), jnp.bfloat16),
        ],
        name="attention_backward",
    )(start, q, g, kv2, kv1, kv0)


def local(queries, keys, values, grad_out, doc_lengths):
    rows, members, width = queries.shape
    heads = lax.axis_size("head")
    kv_heads = width // HD
    assert kv_heads == heads and members == 1
    place = lax.axis_index("head")
    block = lax.axis_index("ctx")
    kv0 = jnp.stack([lax.dynamic_slice_in_dim(a, place * HD, HD, 1) for a in (keys, values)])
    kv1 = shifted(kv0, "ctx", 1)
    kv2 = shifted(kv0, "ctx", 2)

    by_head = jnp.stack([queries, grad_out]).reshape(2, rows, heads, HD).transpose(2, 0, 1, 3)
    mine = lax.all_to_all(by_head, "head", 0, 0, tiled=True)
    q, g = mine[:, 0], mine[:, 1]

    doc_ends = jnp.cumsum(doc_lengths)
    position = block * rows + jnp.arange(rows, dtype=jnp.int32)
    start = jnp.max(jnp.where(doc_ends[:, None] <= position[None, :], doc_ends[:, None], 0), axis=0)
    start = (start - block * rows).astype(jnp.int32)[None, :]

    dq, d2, d1, d0 = attention(start, q, g, kv2, kv1, kv0)
    total = d0 + shifted(d1, "ctx", -1).astype(jnp.float32) + shifted(d2, "ctx", -2).astype(jnp.float32)
    dq = lax.all_to_all(dq, "head", 0, 0, tiled=True)
    query_grad = dq.transpose(1, 0, 2).reshape(rows, 1, width)
    own = rows // heads
    total = total.astype(jnp.bfloat16).reshape(2, heads, own, HD).transpose(1, 0, 2, 3)
    total = lax.all_to_all(total, "head", 0, 0, tiled=True)
    total = total.transpose(1, 2, 0, 3).reshape(2, own, width)
    return (query_grad, total[0], total[1])


def solution(mesh):
    placed = (P("ctx", "head", None), P("ctx", None), P("ctx", None), P("ctx", "head", None), P())
    return jax.shard_map(
        local,
        mesh=mesh,
        in_specs=placed,
        out_specs=(P("ctx", "head", None), P(("ctx", "head"), None), P(("ctx", "head"), None)),
        check_vma=False,
    )
```

```python
import functools
import math

import jax
import jax.numpy as jnp
from jax import lax
from jax.experimental import pallas as pl
from jax.experimental.pallas import tpu as pltpu
from jax.sharding import PartitionSpec as P


HD = 128
HOPS = 2
LOG2E = math.log2(math.e)
NEG = -1e30
TQ = 128
TK = 128
ORDER = (("S0",), ("X0", "S1"), ("P0", "X1"), ("D0", "V0"), ("P1", "K0"), ("V1",), ("D1", "K1"))
VMEM_LIMIT = 24 * 2**20


def rotated(value, axis, steps):
    count = lax.axis_size(axis)
    return lax.ppermute(value, axis, [(source, (source + steps) % count) for source in range(count)])


def shifted(value, axis, steps):
    count = lax.axis_size(axis)
    pairs = [(source, source + steps) for source in range(count) if 0 <= source + steps < count]
    return lax.ppermute(value, axis, pairs)


def swapped(value, axis, bits):
    return lax.ppermute(value, axis, [(source, source ^ bits) for source in range(lax.axis_size(axis))])


def nt(a, b):
    return lax.dot_general(a, b, (((1,), (1,)), ((), ())), preferred_element_type=jnp.float32)


def nn(a, b):
    return lax.dot_general(a, b, (((1,), (0,)), ((), ())), preferred_element_type=jnp.float32)


def call(body, out_shape, in_specs, out_specs, scratch_shapes):
    return pl.pallas_call(
        body,
        out_shape=out_shape,
        in_specs=in_specs,
        out_specs=out_specs,
        scratch_shapes=scratch_shapes,
        compiler_params=pltpu.CompilerParams(vmem_limit_bytes=VMEM_LIMIT),
    )


HBM = pl.BlockSpec(memory_space=pltpu.HBM)
VMEM = pl.BlockSpec(memory_space=pltpu.VMEM)
SMEM = pl.BlockSpec(memory_space=pltpu.SMEM)


def columns(index):
    return pl.ds(pl.multiple_of(index * HD, HD), HD)


def pack_body(place_ref, q_ref, g_ref, k_ref, v_ref, k0_ref, v0_ref, *rest):
    pieces, sems = rest[:-1], rest[-1]
    place = place_ref[0]
    copies = [(k_ref.at[:, columns(place)], k0_ref), (v_ref.at[:, columns(place)], v0_ref)]
    for bits, piece in enumerate(pieces):
        for which, ref in enumerate((q_ref, g_ref)):
            copies.append((ref.at[:, columns(place ^ bits)], piece.at[which]))
    copies = [pltpu.make_async_copy(a, b, sems.at[i]) for i, (a, b) in enumerate(copies)]
    for copy in copies:
        copy.start()
    for copy in copies:
        copy.wait()


def pack(place, q, g, k, v):
    rows, width = q.shape
    heads = width // HD
    block = jax.ShapeDtypeStruct((rows, HD), q.dtype)
    piece = jax.ShapeDtypeStruct((2, rows, HD), q.dtype)
    return call(
        pack_body, (block,) * 2 + (piece,) * heads, [SMEM] + [HBM] * 4, (VMEM,) * (2 + heads),
        [pltpu.SemaphoreType.DMA((2 * (heads + 1),))],
    )(place, q, g, k, v)


def attention_body(scale, bias_ref, *rest):
    blocks = HOPS + 1
    key_blocks, value_blocks, rest = rest[:blocks], rest[blocks : 2 * blocks], rest[2 * blocks :]
    *qg_refs, ds_ref, k_scr = rest[: -6 - blocks]
    d_refs, (v_scr, s_scr, p_scr, dp_scr, dk_acc, dv_acc) = rest[-6 - blocks : -6], rest[-6:]
    rows, _ = key_blocks[-1].shape
    heads, tq, lanes = len(qg_refs), TQ, 2 * TQ
    pairs, tiles = heads // 2, rows // tq
    span = HOPS * rows + tq
    chunks = list(range(0, span, TK))
    c = scale * LOG2E
    for index in range(blocks):
        part = slice(index * rows, (index + 1) * rows)
        k_scr[part, :], v_scr[part, :] = key_blocks[index][...], value_blocks[index][...]
    dk_acc[...] = jnp.zeros_like(dk_acc)
    dv_acc[...] = jnp.zeros_like(dv_acc)

    def fold(x):
        return x.reshape(TK // 8, 8, lanes)

    def one_tile(tile, carry):
        off = pl.multiple_of(tile * tq, tq)
        part = pl.ds(off, tq)
        top, total, delta, q, goq = {}, {}, {}, {}, {}

        def rows_of(j):
            return slice(j, j + TK)

        def window(j):
            return pl.ds(off + j, TK)

        def load(i):
            q[i] = jnp.concatenate([qg_refs[2 * i + half][0, part, :] for half in range(2)], axis=0)
            top[i] = jnp.full((8, lanes), NEG, jnp.float32)
            total[i] = delta[i] = jnp.zeros((8, lanes), jnp.float32)

        def score(i, j):
            b = bias_ref[tile, rows_of(j), :]
            s = nt(k_scr[window(j), :], q[i]) + jnp.concatenate([b, b], axis=1)
            s_scr[i, rows_of(j), :] = s
            top[i] = jnp.maximum(top[i], jnp.max(fold(s), axis=0))

        def exps(i, j):
            if j == 0:
                top[i] = jnp.max(top[i], axis=0, keepdims=True)
            p = jnp.exp2((s_scr[i, rows_of(j), :] - top[i]) * c)
            total[i] = total[i] + jnp.sum(fold(p), axis=0)
            s_scr[i, rows_of(j), :] = p
            p_scr[i, rows_of(j), :] = p.astype(jnp.bfloat16)

        def grads(i, j):
            if j == 0:
                total[i] = 1.0 / jnp.sum(total[i], axis=0, keepdims=True)
                gt = jnp.concatenate([qg_refs[2 * i + half][1, part, :].T for half in range(2)], axis=1)
                goq[i] = (gt.astype(jnp.float32) * total[i]).astype(jnp.bfloat16)
            dp = nn(v_scr[window(j), :], goq[i])
            dp_scr[i, rows_of(j), :] = dp
            delta[i] = delta[i] + jnp.sum(fold(s_scr[i, rows_of(j), :] * dp), axis=0)

        def diffs(i, j):
            if j == 0:
                delta[i] = jnp.sum(delta[i], axis=0, keepdims=True) * total[i]
            ds = s_scr[i, rows_of(j), :] * (dp_scr[i, rows_of(j), :] - delta[i])
            ds_ref[tile * pairs + i, rows_of(j), :] = ds.astype(jnp.bfloat16)

        def value(i, j):
            dv_acc[window(j), :] += nt(p_scr[i, rows_of(j), :], goq[i])

        def key(i, j):
            dk_acc[window(j), :] += nn(ds_ref[tile * pairs + i, rows_of(j), :], q[i])

        ops = {"S": score, "X": exps, "P": grads, "D": diffs, "V": value, "K": key}
        for i in range(pairs):
            load(i)
        for group in ORDER:
            members = [(ops[name[0]], int(name[1])) for name in group]
            for j in chunks:
                for op, i in members:
                    op(i, j)
        return carry

    lax.fori_loop(0, tiles, one_tile, 0)
    for index, ref in enumerate(d_refs):
        part = slice(index * rows, (index + 1) * rows)
        ref[0] = (dk_acc[part, :] * scale).astype(ref.dtype)
        ref[1] = dv_acc[part, :].astype(ref.dtype)


def attention(bias, key_blocks, value_blocks, pieces):
    rows, hd = key_blocks[-1].shape
    pairs = len(pieces) // 2
    steps = pairs * (rows // TQ)
    span, window, lanes = HOPS * rows + TQ, (HOPS + 1) * rows, 2 * TQ
    halo = jax.ShapeDtypeStruct((2, rows, hd), jnp.bfloat16)
    own = jax.ShapeDtypeStruct((2, rows, hd), jnp.float32)
    ds = jax.ShapeDtypeStruct((steps, span, lanes), jnp.bfloat16)
    keys = jax.ShapeDtypeStruct((window, hd), jnp.bfloat16)
    return call(
        functools.partial(attention_body, 1.0 / math.sqrt(hd)),
        (ds, keys) + (halo,) * HOPS + (own,),
        [VMEM] * (1 + 2 * (HOPS + 1) + len(pieces)),
        (VMEM,) * (3 + HOPS),
        [
            pltpu.VMEM((window, hd), jnp.bfloat16),
            pltpu.VMEM((pairs, span, lanes), jnp.float32),
            pltpu.VMEM((pairs, span, lanes), jnp.bfloat16),
            pltpu.VMEM((pairs, span, lanes), jnp.float32),
            pltpu.VMEM((window, hd), jnp.float32),
            pltpu.VMEM((window, hd), jnp.float32),
        ],
    )(bias, *key_blocks, *value_blocks, *pieces)


def query_body(scale, ds_ref, keys_ref, *rest):
    dq_refs, kt_scr = rest[:-1], rest[-1]
    steps, span, lanes = ds_ref.shape
    pairs, tq = len(dq_refs) // 2, lanes // 2
    kt_scr[...] = keys_ref[...].T
    for step in range(steps):
        tile, pair = step // pairs, step % pairs
        dq = (nn(kt_scr[:, tile * tq : tile * tq + span], ds_ref[step]) * scale).T.astype(jnp.bfloat16)
        for half in range(2):
            dq_refs[2 * pair + half][tile * tq : (tile + 1) * tq, :] = dq[half * tq : (half + 1) * tq, :]


def query_part(ds, keys, rows, heads):
    window, hd = keys.shape
    return call(
        functools.partial(query_body, 1.0 / math.sqrt(hd)),
        (jax.ShapeDtypeStruct((rows, hd), jnp.bfloat16),) * heads,
        [VMEM] * 2, (VMEM,) * heads, [pltpu.VMEM((hd, window), jnp.bfloat16)],
    )(ds, keys)


def bias_body(block_ref, lengths_ref, bias_ref):
    tiles, span, tq = bias_ref.shape
    back = span - tq
    first = block_ref[0] * (tiles * tq)
    position = lax.broadcasted_iota(jnp.int32, (8, tiles * tq), 1)

    def one_document(index, carry):
        end, start = carry
        end = end + lengths_ref[index]
        return end, jnp.where(position >= end, end, start)

    opening = (-first, jnp.full(position.shape, -first, jnp.int32))
    _, starts = lax.fori_loop(0, lengths_ref.shape[0], one_document, opening)
    for tile in range(tiles):
        start = starts[:1, tile * tq : (tile + 1) * tq]
        for j in range(0, span, tq):
            t = lax.broadcasted_iota(jnp.int32, (tq, tq), 0) + (tile * tq + j - back)
            allowed = t >= start
            if j == back:
                allowed &= t <= lax.broadcasted_iota(jnp.int32, (tq, tq), 1) + tile * tq
            bias_ref[tile, j : j + tq, :] = jnp.where(allowed, 0.0, NEG)


def make_bias(block, lengths, rows):
    out = jax.ShapeDtypeStruct((rows // TQ, HOPS * rows + TQ, TQ), jnp.float32)
    return call(bias_body, out, [SMEM] * 2, VMEM, [])(block, lengths)


def choose_body(odd_ref, even_value_ref, odd_value_ref, out_ref):
    odd = odd_ref[0] == 1

    @pl.when(odd)
    def _():
        out_ref[...] = odd_value_ref[...]

    @pl.when(jnp.logical_not(odd))
    def _():
        out_ref[...] = even_value_ref[...]


def choose(odd, even_value, odd_value):
    out = jax.ShapeDtypeStruct(even_value.shape, even_value.dtype)
    return call(choose_body, out, [SMEM] + [VMEM] * 2, VMEM, [])(odd, even_value, odd_value)


def join_body(place_ref, d0_ref, r1_ref, r2_ref, *out_refs):
    place = place_ref[0]
    own = out_refs[0].shape[1]
    for bits, ref in enumerate(out_refs):
        part = pl.ds(pl.multiple_of((place ^ bits) * own, own), own)
        total = d0_ref[:, part, :] + r1_ref[:, part, :].astype(jnp.float32) + r2_ref[:, part, :].astype(jnp.float32)
        ref[...] = total.astype(ref.dtype)


def join(place, d0, r1, r2, heads):
    _, rows, hd = d0.shape
    piece = jax.ShapeDtypeStruct((2, rows // heads, hd), jnp.bfloat16)
    return call(join_body, (piece,) * heads, [SMEM] + [VMEM] * 3, (VMEM,) * heads, [])(place, d0, r1, r2)


def spread_body(place_ref, *refs):
    place = place_ref[0]
    pieces, out_ref = refs[:-1], refs[-1]
    for bits, ref in enumerate(pieces):
        out_ref[:, columns(place ^ bits)] = ref[...]


def spread(place, pieces):
    rows, hd = pieces[0].shape
    out = jax.ShapeDtypeStruct((rows, hd * len(pieces)), pieces[0].dtype)
    return call(spread_body, out, [SMEM] + [VMEM] * len(pieces), VMEM, [])(place, *pieces)


def spread_pair_body(place_ref, *refs):
    place = place_ref[0]
    pieces, out_refs = refs[:-2], refs[-2:]
    for bits, ref in enumerate(pieces):
        for which, out_ref in enumerate(out_refs):
            out_ref[:, columns(place ^ bits)] = ref[which]


def spread_pair(place, pieces):
    _, rows, hd = pieces[0].shape
    out = jax.ShapeDtypeStruct((rows, hd * len(pieces)), pieces[0].dtype)
    return call(spread_pair_body, (out, out), [SMEM] + [VMEM] * len(pieces), (VMEM, VMEM), [])(place, *pieces)


def local(queries, keys, values, grad_out, doc_lengths):
    rows, members, width = queries.shape
    heads = lax.axis_size("head")
    assert width // HD == heads and members == 1
    place = lax.axis_index("head").astype(jnp.int32)[None]
    block = lax.axis_index("ctx")
    assert lax.axis_size("ctx") % 2 == 0
    odd = (block % 2).astype(jnp.int32)[None]
    whole = [queries.reshape(rows, width), grad_out.reshape(rows, width), keys, values]
    whole = [pltpu.with_memory_space_constraint(a, pltpu.HBM) for a in whole]
    k0, v0, *pieces = pack(place, *whole)
    k2 = rotated(k0, "ctx", 2)
    v2 = rotated(v0, "ctx", 2)
    k1 = swapped(choose(odd, k0, k2), "ctx", 1)
    v1 = swapped(choose(odd, v0, v2), "ctx", 1)
    pieces = [pieces[0]] + [swapped(pieces[bits], "head", bits) for bits in range(1, heads)]

    bias = make_bias(block.astype(jnp.int32)[None], doc_lengths, rows)
    ds, window_keys, d2, d1, d0 = attention(bias, (k2, k1, k0), (v2, v1, v0), pieces)
    r2 = rotated(d2, "ctx", -2)
    r1 = shifted(d1, "ctx", -1)
    dq = query_part(ds, window_keys, rows, heads)
    dq = [dq[0]] + [swapped(dq[bits], "head", bits) for bits in range(1, heads)]
    query_grad = spread(place, dq).reshape(rows, 1, width)
    parts = join(place, d0, r1, r2, heads)
    parts = [parts[0]] + [swapped(parts[bits], "head", bits) for bits in range(1, heads)]
    key_grad, value_grad = spread_pair(place, parts)
    return (query_grad, key_grad, value_grad)


def solution(mesh):
    placed = (P("ctx", "head", None), P("ctx", None), P("ctx", None), P("ctx", "head", None), P())
    return jax.shard_map(
        local,
        mesh=mesh,
        in_specs=placed,
        out_specs=(P("ctx", "head", None), P(("ctx", "head"), None), P(("ctx", "head"), None)),
        check_vma=False,
    )
```

```python
import functools
import math

import jax
import jax.numpy as jnp
from jax import lax
from jax.experimental import pallas as pl
from jax.experimental.pallas import tpu as pltpu
from jax.sharding import PartitionSpec as P


HD = 128
HOPS = 2
LOG2E = math.log2(math.e)
NEG = -1e30
TQ = 128
TK = 576
ORDER = (("S0",), ("X0",), ("S1",), ("P0",), ("D0",), ("X1",), ("V0",), ("P1",), ("D1",), ("K0",), ("V1",), ("K1",))
VMEM_LIMIT = 24 * 2**20


def rotated(value, axis, steps):
    count = lax.axis_size(axis)
    return lax.ppermute(value, axis, [(source, (source + steps) % count) for source in range(count)])


def shifted(value, axis, steps):
    count = lax.axis_size(axis)
    pairs = [(source, source + steps) for source in range(count) if 0 <= source + steps < count]
    return lax.ppermute(value, axis, pairs)


def swapped(value, axis, bits):
    return lax.ppermute(value, axis, [(source, source ^ bits) for source in range(lax.axis_size(axis))])


def nt(a, b):
    return lax.dot_general(a, b, (((1,), (1,)), ((), ())), preferred_element_type=jnp.float32)


def nn(a, b):
    return lax.dot_general(a, b, (((1,), (0,)), ((), ())), preferred_element_type=jnp.float32)


def call(body, out_shape, in_specs, out_specs, scratch_shapes):
    return pl.pallas_call(
        body,
        out_shape=out_shape,
        in_specs=in_specs,
        out_specs=out_specs,
        scratch_shapes=scratch_shapes,
        compiler_params=pltpu.CompilerParams(vmem_limit_bytes=VMEM_LIMIT),
    )


HBM = pl.BlockSpec(memory_space=pltpu.HBM)
VMEM = pl.BlockSpec(memory_space=pltpu.VMEM)
SMEM = pl.BlockSpec(memory_space=pltpu.SMEM)


def columns(index):
    return pl.ds(pl.multiple_of(index * HD, HD), HD)


def pack_body(place_ref, q_ref, g_ref, k_ref, v_ref, k0_ref, v0_ref, *rest):
    pieces, sems = rest[:-1], rest[-1]
    place = place_ref[0]
    copies = [(k_ref.at[:, columns(place)], k0_ref), (v_ref.at[:, columns(place)], v0_ref)]
    for bits, piece in enumerate(pieces):
        for which, ref in enumerate((q_ref, g_ref)):
            copies.append((ref.at[:, columns(place ^ bits)], piece.at[which]))
    copies = [pltpu.make_async_copy(a, b, sems.at[i]) for i, (a, b) in enumerate(copies)]
    for copy in copies:
        copy.start()
    for copy in copies:
        copy.wait()


def pack(place, q, g, k, v):
    rows, width = q.shape
    heads = width // HD
    block = jax.ShapeDtypeStruct((rows, HD), q.dtype)
    piece = jax.ShapeDtypeStruct((2, rows, HD), q.dtype)
    return call(
        pack_body, (block,) * 2 + (piece,) * heads, [SMEM] + [HBM] * 4, (VMEM,) * (2 + heads),
        [pltpu.SemaphoreType.DMA((2 * (heads + 1),))],
    )(place, q, g, k, v)


def attention_body(scale, bias_ref, *rest):
    blocks = HOPS + 1
    key_blocks, value_blocks, rest = rest[:blocks], rest[blocks : 2 * blocks], rest[2 * blocks :]
    *qg_refs, ds_ref, k_scr = rest[: -6 - blocks]
    d_refs, (v_scr, s_scr, p_scr, vt_scr, dk_acc, dv_acc) = rest[-6 - blocks : -6], rest[-6:]
    rows, _ = key_blocks[-1].shape
    heads, tq, lanes = len(qg_refs), TQ, 2 * TQ
    pairs, tiles = heads // 2, rows // tq
    span = HOPS * rows + tq
    chunks = list(range(0, span, TK))
    c = scale * LOG2E
    for index in range(blocks):
        part = slice(index * rows, (index + 1) * rows)
        k_scr[part, :], v_scr[part, :] = key_blocks[index][...], value_blocks[index][...]
        vt_scr[:, part] = value_blocks[index][...].T
    dk_acc[...] = jnp.zeros_like(dk_acc)
    dv_acc[...] = jnp.zeros_like(dv_acc)

    def fold(x):
        return x.reshape(TK // 8, 8, lanes)

    def one_tile(tile, carry):
        off = pl.multiple_of(tile * tq, tq)
        part = pl.ds(off, tq)
        top, total, delta, q, goq = {}, {}, {}, {}, {}

        def rows_of(j):
            return slice(j, j + TK)

        def window(j):
            return pl.ds(off + j, TK)

        def load(i):
            q[i] = jnp.concatenate([qg_refs[2 * i + half][0, part, :] for half in range(2)], axis=0)
            top[i] = jnp.full((8, lanes), NEG, jnp.float32)
            total[i] = delta[i] = jnp.zeros((8, lanes), jnp.float32)

        def score(i, j):
            b = bias_ref[tile, rows_of(j), :]
            s = nt(k_scr[window(j), :], q[i]) + jnp.concatenate([b, b], axis=1)
            s_scr[i, rows_of(j), :] = s
            top[i] = jnp.maximum(top[i], jnp.max(fold(s), axis=0))

        def exps(i, j):
            if j == 0:
                top[i] = jnp.max(top[i], axis=0, keepdims=True)
            p = jnp.exp2((s_scr[i, rows_of(j), :] - top[i]) * c)
            total[i] = total[i] + jnp.sum(fold(p), axis=0)
            s_scr[i, rows_of(j), :] = p
            p_scr[i, rows_of(j), :] = p.astype(jnp.bfloat16)

        def grads(i, j):
            if j == 0:
                total[i] = 1.0 / jnp.sum(total[i], axis=0, keepdims=True)
                gt = jnp.concatenate([qg_refs[2 * i + half][1, part, :].T for half in range(2)], axis=1)
                goq[i] = (gt.astype(jnp.float32) * total[i]).astype(jnp.bfloat16)
                out = nn(vt_scr[:, pl.ds(off, span)], p_scr[i])
                delta[i] = jnp.sum(goq[i].astype(jnp.float32) * out, axis=0, keepdims=True) * total[i]

        def diffs(i, j):
            dp = nn(v_scr[window(j), :], goq[i])
            ds = s_scr[i, rows_of(j), :] * (dp - delta[i])
            ds_ref[tile * pairs + i, rows_of(j), :] = ds.astype(jnp.bfloat16)

        def value(i, j):
            dv_acc[window(j), :] += nt(p_scr[i, rows_of(j), :], goq[i])

        def key(i, j):
            dk_acc[window(j), :] += nn(ds_ref[tile * pairs + i, rows_of(j), :], q[i])

        ops = {"S": score, "X": exps, "P": grads, "D": diffs, "V": value, "K": key}
        for i in range(pairs):
            load(i)
        for group in ORDER:
            members = [(ops[name[0]], int(name[1])) for name in group]
            for j in chunks:
                for op, i in members:
                    op(i, j)
        return carry

    lax.fori_loop(0, tiles, one_tile, 0)
    for index, ref in enumerate(d_refs):
        part = slice(index * rows, (index + 1) * rows)
        ref[0] = (dk_acc[part, :] * scale).astype(ref.dtype)
        ref[1] = dv_acc[part, :].astype(ref.dtype)


def attention(bias, key_blocks, value_blocks, pieces):
    rows, hd = key_blocks[-1].shape
    pairs = len(pieces) // 2
    steps = pairs * (rows // TQ)
    span, window, lanes = HOPS * rows + TQ, (HOPS + 1) * rows, 2 * TQ
    halo = jax.ShapeDtypeStruct((2, rows, hd), jnp.bfloat16)
    own = jax.ShapeDtypeStruct((2, rows, hd), jnp.float32)
    ds = jax.ShapeDtypeStruct((steps, span, lanes), jnp.bfloat16)
    keys = jax.ShapeDtypeStruct((window, hd), jnp.bfloat16)
    return call(
        functools.partial(attention_body, 1.0 / math.sqrt(hd)),
        (ds, keys) + (halo,) * HOPS + (own,),
        [VMEM] * (1 + 2 * (HOPS + 1) + len(pieces)),
        (VMEM,) * (3 + HOPS),
        [
            pltpu.VMEM((window, hd), jnp.bfloat16),
            pltpu.VMEM((pairs, span, lanes), jnp.float32),
            pltpu.VMEM((pairs, span, lanes), jnp.bfloat16),
            pltpu.VMEM((hd, window), jnp.bfloat16),
            pltpu.VMEM((window, hd), jnp.float32),
            pltpu.VMEM((window, hd), jnp.float32),
        ],
    )(bias, *key_blocks, *value_blocks, *pieces)


def query_body(scale, ds_ref, keys_ref, *rest):
    dq_refs, kt_scr = rest[:-1], rest[-1]
    steps, span, lanes = ds_ref.shape
    pairs, tq = len(dq_refs) // 2, lanes // 2
    kt_scr[...] = keys_ref[...].T
    for step in range(steps):
        tile, pair = step // pairs, step % pairs
        dq = (nn(kt_scr[:, tile * tq : tile * tq + span], ds_ref[step]) * scale).T.astype(jnp.bfloat16)
        for half in range(2):
            dq_refs[2 * pair + half][tile * tq : (tile + 1) * tq, :] = dq[half * tq : (half + 1) * tq, :]


def query_part(ds, keys, rows, heads):
    window, hd = keys.shape
    return call(
        functools.partial(query_body, 1.0 / math.sqrt(hd)),
        (jax.ShapeDtypeStruct((rows, hd), jnp.bfloat16),) * heads,
        [VMEM] * 2, (VMEM,) * heads, [pltpu.VMEM((hd, window), jnp.bfloat16)],
    )(ds, keys)


def bias_body(block_ref, lengths_ref, bias_ref):
    tiles, span, tq = bias_ref.shape
    back = span - tq
    first = block_ref[0] * (tiles * tq)
    position = lax.broadcasted_iota(jnp.int32, (8, tiles * tq), 1)

    def one_document(index, carry):
        end, start = carry
        end = end + lengths_ref[index]
        return end, jnp.where(position >= end, end, start)

    opening = (-first, jnp.full(position.shape, -first, jnp.int32))
    _, starts = lax.fori_loop(0, lengths_ref.shape[0], one_document, opening)
    for tile in range(tiles):
        start = starts[:1, tile * tq : (tile + 1) * tq]
        for j in range(0, span, tq):
            t = lax.broadcasted_iota(jnp.int32, (tq, tq), 0) + (tile * tq + j - back)
            allowed = t >= start
            if j == back:
                allowed &= t <= lax.broadcasted_iota(jnp.int32, (tq, tq), 1) + tile * tq
            bias_ref[tile, j : j + tq, :] = jnp.where(allowed, 0.0, NEG)


def make_bias(block, lengths, rows):
    out = jax.ShapeDtypeStruct((rows // TQ, HOPS * rows + TQ, TQ), jnp.float32)
    return call(bias_body, out, [SMEM] * 2, VMEM, [])(block, lengths)


def choose_body(odd_ref, even_value_ref, odd_value_ref, out_ref):
    odd = odd_ref[0] == 1

    @pl.when(odd)
    def _():
        out_ref[...] = odd_value_ref[...]

    @pl.when(jnp.logical_not(odd))
    def _():
        out_ref[...] = even_value_ref[...]


def choose(odd, even_value, odd_value):
    out = jax.ShapeDtypeStruct(even_value.shape, even_value.dtype)
    return call(choose_body, out, [SMEM] + [VMEM] * 2, VMEM, [])(odd, even_value, odd_value)


def join_body(place_ref, d0_ref, r1_ref, r2_ref, *out_refs):
    place = place_ref[0]
    own = out_refs[0].shape[1]
    for bits, ref in enumerate(out_refs):
        part = pl.ds(pl.multiple_of((place ^ bits) * own, own), own)
        total = d0_ref[:, part, :] + r1_ref[:, part, :].astype(jnp.float32) + r2_ref[:, part, :].astype(jnp.float32)
        ref[...] = total.astype(ref.dtype)


def join(place, d0, r1, r2, heads):
    _, rows, hd = d0.shape
    piece = jax.ShapeDtypeStruct((2, rows // heads, hd), jnp.bfloat16)
    return call(join_body, (piece,) * heads, [SMEM] + [VMEM] * 3, (VMEM,) * heads, [])(place, d0, r1, r2)


def spread_body(place_ref, *refs):
    place = place_ref[0]
    pieces, out_ref = refs[:-1], refs[-1]
    for bits, ref in enumerate(pieces):
        out_ref[:, columns(place ^ bits)] = ref[...]


def spread(place, pieces):
    rows, hd = pieces[0].shape
    out = jax.ShapeDtypeStruct((rows, hd * len(pieces)), pieces[0].dtype)
    return call(spread_body, out, [SMEM] + [VMEM] * len(pieces), VMEM, [])(place, *pieces)


def spread_pair_body(place_ref, *refs):
    place = place_ref[0]
    pieces, out_refs = refs[:-2], refs[-2:]
    for bits, ref in enumerate(pieces):
        for which, out_ref in enumerate(out_refs):
            out_ref[:, columns(place ^ bits)] = ref[which]


def spread_pair(place, pieces):
    _, rows, hd = pieces[0].shape
    out = jax.ShapeDtypeStruct((rows, hd * len(pieces)), pieces[0].dtype)
    return call(spread_pair_body, (out, out), [SMEM] + [VMEM] * len(pieces), (VMEM, VMEM), [])(place, *pieces)


def local(queries, keys, values, grad_out, doc_lengths):
    rows, members, width = queries.shape
    heads = lax.axis_size("head")
    assert width // HD == heads and members == 1
    place = lax.axis_index("head").astype(jnp.int32)[None]
    block = lax.axis_index("ctx")
    assert lax.axis_size("ctx") % 2 == 0
    odd = (block % 2).astype(jnp.int32)[None]
    whole = [queries.reshape(rows, width), grad_out.reshape(rows, width), keys, values]
    whole = [pltpu.with_memory_space_constraint(a, pltpu.HBM) for a in whole]
    k0, v0, *pieces = pack(place, *whole)
    k2 = rotated(k0, "ctx", 2)
    v2 = rotated(v0, "ctx", 2)
    k1 = swapped(choose(odd, k0, k2), "ctx", 1)
    v1 = swapped(choose(odd, v0, v2), "ctx", 1)
    pieces = [pieces[0]] + [swapped(pieces[bits], "head", bits) for bits in range(1, heads)]

    bias = make_bias(block.astype(jnp.int32)[None], doc_lengths, rows)
    ds, window_keys, d2, d1, d0 = attention(bias, (k2, k1, k0), (v2, v1, v0), pieces)
    r2 = rotated(d2, "ctx", -2)
    r1 = shifted(d1, "ctx", -1)
    dq = query_part(ds, window_keys, rows, heads)
    dq = [dq[0]] + [swapped(dq[bits], "head", bits) for bits in range(1, heads)]
    query_grad = spread(place, dq).reshape(rows, 1, width)
    parts = join(place, d0, r1, r2, heads)
    parts = [parts[0]] + [swapped(parts[bits], "head", bits) for bits in range(1, heads)]
    key_grad, value_grad = spread_pair(place, parts)
    return (query_grad, key_grad, value_grad)


def solution(mesh):
    placed = (P("ctx", "head", None), P("ctx", None), P("ctx", None), P("ctx", "head", None), P())
    return jax.shard_map(
        local,
        mesh=mesh,
        in_specs=placed,
        out_specs=(P("ctx", "head", None), P(("ctx", "head"), None), P(("ctx", "head"), None)),
        check_vma=False,
    )
```

```python
import functools
import math

import jax
import jax.numpy as jnp
from jax import lax
from jax.experimental import pallas as pl
from jax.experimental.pallas import tpu as pltpu
from jax.sharding import PartitionSpec as P


HD = 128
HOPS = 2
LOG2E = math.log2(math.e)
NEG = -1e30
TQ = 128
TK = 576
ORDER = (("S0",), ("X0",), ("S1",), ("P0",), ("D0",), ("X1",), ("V0",), ("P1",), ("D1",), ("K0",), ("V1",), ("K1",))
VMEM_LIMIT = 24 * 2**20


def rotated(value, axis, steps):
    count = lax.axis_size(axis)
    return lax.ppermute(value, axis, [(source, (source + steps) % count) for source in range(count)])


def shifted(value, axis, steps):
    count = lax.axis_size(axis)
    pairs = [(source, source + steps) for source in range(count) if 0 <= source + steps < count]
    return lax.ppermute(value, axis, pairs)


def swapped(value, axis, bits):
    return lax.ppermute(value, axis, [(source, source ^ bits) for source in range(lax.axis_size(axis))])


def nt(a, b):
    return lax.dot_general(a, b, (((1,), (1,)), ((), ())), preferred_element_type=jnp.float32)


def nn(a, b):
    return lax.dot_general(a, b, (((1,), (0,)), ((), ())), preferred_element_type=jnp.float32)


def call(body, out_shape, in_specs, out_specs, scratch_shapes):
    return pl.pallas_call(
        body,
        out_shape=out_shape,
        in_specs=in_specs,
        out_specs=out_specs,
        scratch_shapes=scratch_shapes,
        compiler_params=pltpu.CompilerParams(vmem_limit_bytes=VMEM_LIMIT),
    )


HBM = pl.BlockSpec(memory_space=pltpu.HBM)
VMEM = pl.BlockSpec(memory_space=pltpu.VMEM)
SMEM = pl.BlockSpec(memory_space=pltpu.SMEM)


def columns(index):
    return pl.ds(pl.multiple_of(index * HD, HD), HD)


def pack_body(plan, place_ref, *refs):
    place = place_ref[0]
    wholes, pieces, sems = refs[:4], refs[4:-1], refs[-1]
    copies = []
    for (first, bits), piece in zip(plan, pieces):
        if first < 2:
            copies.append((wholes[2 + first].at[:, columns(place)], piece))
        else:
            copies += [(wholes[i].at[:, columns(place ^ bits)], piece.at[i]) for i in range(2)]
    copies = [pltpu.make_async_copy(a, b, sems.at[i]) for i, (a, b) in enumerate(copies)]
    for copy in copies:
        copy.start()
    for copy in copies:
        copy.wait()


def pack(plan, place, *wholes):
    rows = wholes[0].shape[0]
    shapes = [(rows, HD) if first < 2 else (2, rows, HD) for first, _ in plan]
    return call(
        functools.partial(pack_body, plan),
        tuple(jax.ShapeDtypeStruct(shape, jnp.bfloat16) for shape in shapes),
        [SMEM] + [HBM] * 4, (VMEM,) * len(plan), [pltpu.SemaphoreType.DMA((2 * len(plan),))],
    )(place, *wholes)


def attention_body(scale, bias_ref, *rest):
    blocks = HOPS + 1
    key_blocks, value_blocks, rest = rest[:blocks], rest[blocks : 2 * blocks], rest[2 * blocks :]
    *qg_refs, ds_ref, k_scr = rest[: -6 - blocks]
    d_refs, (v_scr, s_scr, p_scr, vt_scr, dk_acc, dv_acc) = rest[-6 - blocks : -6], rest[-6:]
    rows, _ = key_blocks[-1].shape
    heads, tq, lanes = len(qg_refs), TQ, 2 * TQ
    pairs, tiles = heads // 2, rows // tq
    span = HOPS * rows + tq
    chunks = list(range(0, span, TK))
    c = scale * LOG2E
    for index in range(blocks):
        part = slice(index * rows, (index + 1) * rows)
        k_scr[part, :], v_scr[part, :] = key_blocks[index][...], value_blocks[index][...]
        vt_scr[:, part] = value_blocks[index][...].T
    dk_acc[...] = jnp.zeros_like(dk_acc)
    dv_acc[...] = jnp.zeros_like(dv_acc)

    def fold(x):
        return x.reshape(TK // 8, 8, lanes)

    def one_tile(tile, carry):
        off = pl.multiple_of(tile * tq, tq)
        part = pl.ds(off, tq)
        top, total, delta, q, goq = {}, {}, {}, {}, {}

        def rows_of(j):
            return slice(j, j + TK)

        def window(j):
            return pl.ds(off + j, TK)

        def load(i):
            q[i] = jnp.concatenate([qg_refs[2 * i + half][0, part, :] for half in range(2)], axis=0)
            top[i] = jnp.full((8, lanes), NEG, jnp.float32)
            total[i] = delta[i] = jnp.zeros((8, lanes), jnp.float32)

        def score(i, j):
            b = bias_ref[tile, rows_of(j), :]
            s = nt(k_scr[window(j), :], q[i]) + jnp.concatenate([b, b], axis=1)
            s_scr[i, rows_of(j), :] = s
            top[i] = jnp.maximum(top[i], jnp.max(fold(s), axis=0))

        def exps(i, j):
            if j == 0:
                top[i] = jnp.max(top[i], axis=0, keepdims=True)
            p = jnp.exp2((s_scr[i, rows_of(j), :] - top[i]) * c)
            total[i] = total[i] + jnp.sum(fold(p), axis=0)
            s_scr[i, rows_of(j), :] = p
            p_scr[i, rows_of(j), :] = p.astype(jnp.bfloat16)

        def grads(i, j):
            if j == 0:
                total[i] = 1.0 / jnp.sum(total[i], axis=0, keepdims=True)
                gt = jnp.concatenate([qg_refs[2 * i + half][1, part, :].T for half in range(2)], axis=1)
                goq[i] = (gt.astype(jnp.float32) * total[i]).astype(jnp.bfloat16)
                out = nn(vt_scr[:, pl.ds(off, span)], p_scr[i])
                delta[i] = jnp.sum(goq[i].astype(jnp.float32) * out, axis=0, keepdims=True) * total[i]

        def diffs(i, j):
            dp = nn(v_scr[window(j), :], goq[i])
            ds = s_scr[i, rows_of(j), :] * (dp - delta[i])
            ds_ref[tile * pairs + i, rows_of(j), :] = ds.astype(jnp.bfloat16)

        def value(i, j):
            dv_acc[window(j), :] += nt(p_scr[i, rows_of(j), :], goq[i])

        def key(i, j):
            dk_acc[window(j), :] += nn(ds_ref[tile * pairs + i, rows_of(j), :], q[i])

        ops = {"S": score, "X": exps, "P": grads, "D": diffs, "V": value, "K": key}
        for i in range(pairs):
            load(i)
        for group in ORDER:
            members = [(ops[name[0]], int(name[1])) for name in group]
            for j in chunks:
                for op, i in members:
                    op(i, j)
        return carry

    lax.fori_loop(0, tiles, one_tile, 0)
    for index, ref in enumerate(d_refs):
        part = slice(index * rows, (index + 1) * rows)
        ref[0] = (dk_acc[part, :] * scale).astype(ref.dtype)
        ref[1] = dv_acc[part, :].astype(ref.dtype)


def attention(bias, key_blocks, value_blocks, pieces):
    rows, hd = key_blocks[-1].shape
    pairs = len(pieces) // 2
    steps = pairs * (rows // TQ)
    span, window, lanes = HOPS * rows + TQ, (HOPS + 1) * rows, 2 * TQ
    halo = jax.ShapeDtypeStruct((2, rows, hd), jnp.bfloat16)
    own = jax.ShapeDtypeStruct((2, rows, hd), jnp.float32)
    ds = jax.ShapeDtypeStruct((steps, span, lanes), jnp.bfloat16)
    keys = jax.ShapeDtypeStruct((window, hd), jnp.bfloat16)
    return call(
        functools.partial(attention_body, 1.0 / math.sqrt(hd)),
        (ds, keys) + (halo,) * HOPS + (own,),
        [VMEM] * (1 + 2 * (HOPS + 1) + len(pieces)),
        (VMEM,) * (3 + HOPS),
        [
            pltpu.VMEM((window, hd), jnp.bfloat16),
            pltpu.VMEM((pairs, span, lanes), jnp.float32),
            pltpu.VMEM((pairs, span, lanes), jnp.bfloat16),
            pltpu.VMEM((hd, window), jnp.bfloat16),
            pltpu.VMEM((window, hd), jnp.float32),
            pltpu.VMEM((window, hd), jnp.float32),
        ],
    )(bias, *key_blocks, *value_blocks, *pieces)


def query_body(scale, ds_ref, keys_ref, *rest):
    dq_refs, kt_scr = rest[:-1], rest[-1]
    steps, span, lanes = ds_ref.shape
    pairs, tq = len(dq_refs) // 2, lanes // 2
    kt_scr[...] = keys_ref[...].T
    for step in range(steps):
        tile, pair = step // pairs, step % pairs
        dq = (nn(kt_scr[:, tile * tq : tile * tq + span], ds_ref[step]) * scale).T.astype(jnp.bfloat16)
        for half in range(2):
            dq_refs[2 * pair + half][tile * tq : (tile + 1) * tq, :] = dq[half * tq : (half + 1) * tq, :]


def query_part(ds, keys, rows, heads):
    window, hd = keys.shape
    return call(
        functools.partial(query_body, 1.0 / math.sqrt(hd)),
        (jax.ShapeDtypeStruct((rows, hd), jnp.bfloat16),) * heads,
        [VMEM] * 2, (VMEM,) * heads, [pltpu.VMEM((hd, window), jnp.bfloat16)],
    )(ds, keys)


def bias_body(block_ref, lengths_ref, bias_ref):
    tiles, span, tq = bias_ref.shape
    back = span - tq
    first = block_ref[0] * (tiles * tq)
    position = lax.broadcasted_iota(jnp.int32, (8, tiles * tq), 1)

    def one_document(index, carry):
        end, start = carry
        end = end + lengths_ref[index]
        return end, jnp.where(position >= end, end, start)

    opening = (-first, jnp.full(position.shape, -first, jnp.int32))
    _, starts = lax.fori_loop(0, lengths_ref.shape[0], one_document, opening)
    for tile in range(tiles):
        start = starts[:1, tile * tq : (tile + 1) * tq]
        for j in range(0, span, tq):
            t = lax.broadcasted_iota(jnp.int32, (tq, tq), 0) + (tile * tq + j - back)
            allowed = t >= start
            if j == back:
                allowed &= t <= lax.broadcasted_iota(jnp.int32, (tq, tq), 1) + tile * tq
            bias_ref[tile, j : j + tq, :] = jnp.where(allowed, 0.0, NEG)


def make_bias(block, lengths, rows):
    out = jax.ShapeDtypeStruct((rows // TQ, HOPS * rows + TQ, TQ), jnp.float32)
    return call(bias_body, out, [SMEM] * 2, VMEM, [])(block, lengths)


def choose_body(odd_ref, even_value_ref, odd_value_ref, out_ref):
    odd = odd_ref[0] == 1

    @pl.when(odd)
    def _():
        out_ref[...] = odd_value_ref[...]

    @pl.when(jnp.logical_not(odd))
    def _():
        out_ref[...] = even_value_ref[...]


def choose(odd, even_value, odd_value):
    out = jax.ShapeDtypeStruct(even_value.shape, even_value.dtype)
    return call(choose_body, out, [SMEM] + [VMEM] * 2, VMEM, [])(odd, even_value, odd_value)


def join_body(place_ref, d0_ref, r1_ref, r2_ref, *out_refs):
    place = place_ref[0]
    own = out_refs[0].shape[1]
    for bits, ref in enumerate(out_refs):
        part = pl.ds(pl.multiple_of((place ^ bits) * own, own), own)
        total = d0_ref[:, part, :] + r1_ref[:, part, :].astype(jnp.float32) + r2_ref[:, part, :].astype(jnp.float32)
        ref[...] = total.astype(ref.dtype)


def join(place, d0, r1, r2, heads):
    _, rows, hd = d0.shape
    piece = jax.ShapeDtypeStruct((2, rows // heads, hd), jnp.bfloat16)
    return call(join_body, (piece,) * heads, [SMEM] + [VMEM] * 3, (VMEM,) * heads, [])(place, d0, r1, r2)


def spread_body(place_ref, *refs):
    place = place_ref[0]
    pieces, out_ref = refs[:-1], refs[-1]
    for bits, ref in enumerate(pieces):
        out_ref[:, columns(place ^ bits)] = ref[...]


def spread(place, pieces):
    rows, hd = pieces[0].shape
    out = jax.ShapeDtypeStruct((rows, hd * len(pieces)), pieces[0].dtype)
    return call(spread_body, out, [SMEM] + [VMEM] * len(pieces), VMEM, [])(place, *pieces)


def spread_pair_body(place_ref, *refs):
    place = place_ref[0]
    pieces, out_refs = refs[:-2], refs[-2:]
    for bits, ref in enumerate(pieces):
        for which, out_ref in enumerate(out_refs):
            out_ref[:, columns(place ^ bits)] = ref[which]


def spread_pair(place, pieces):
    _, rows, hd = pieces[0].shape
    out = jax.ShapeDtypeStruct((rows, hd * len(pieces)), pieces[0].dtype)
    return call(spread_pair_body, (out, out), [SMEM] + [VMEM] * len(pieces), (VMEM, VMEM), [])(place, *pieces)


def local(queries, keys, values, grad_out, doc_lengths):
    rows, members, width = queries.shape
    heads = lax.axis_size("head")
    assert width // HD == heads and members == 1
    place = lax.axis_index("head").astype(jnp.int32)[None]
    block = lax.axis_index("ctx")
    assert lax.axis_size("ctx") % 2 == 0
    odd = (block % 2).astype(jnp.int32)[None]
    whole = [queries.reshape(rows, width), grad_out.reshape(rows, width), keys, values]
    whole = [pltpu.with_memory_space_constraint(a, pltpu.HBM) for a in whole]
    k0, far_piece = pack(((0, 0), (2, 2)), place, *whole)
    others = [bits for bits in range(heads) if bits != 2]
    v0, *pieces = pack(((1, 0),) + tuple((2, bits) for bits in others), place, *whole)
    pieces.insert(2, far_piece)
    k2 = rotated(k0, "ctx", 2)
    v2 = rotated(v0, "ctx", 2)
    k1 = swapped(choose(odd, k0, k2), "ctx", 1)
    v1 = swapped(choose(odd, v0, v2), "ctx", 1)
    pieces = [pieces[0]] + [swapped(pieces[bits], "head", bits) for bits in range(1, heads)]

    bias = make_bias(block.astype(jnp.int32)[None], doc_lengths, rows)
    ds, window_keys, d2, d1, d0 = attention(bias, (k2, k1, k0), (v2, v1, v0), pieces)
    r2 = rotated(d2, "ctx", -2)
    r1 = shifted(d1, "ctx", -1)
    dq = query_part(ds, window_keys, rows, heads)
    dq = [dq[0]] + [swapped(dq[bits], "head", bits) for bits in range(1, heads)]
    query_grad = spread(place, dq).reshape(rows, 1, width)
    parts = join(place, d0, r1, r2, heads)
    parts = [parts[0]] + [swapped(parts[bits], "head", bits) for bits in range(1, heads)]
    key_grad, value_grad = spread_pair(place, parts)
    return (query_grad, key_grad, value_grad)


def solution(mesh):
    placed = (P("ctx", "head", None), P("ctx", None), P("ctx", None), P("ctx", "head", None), P())
    return jax.shard_map(
        local,
        mesh=mesh,
        in_specs=placed,
        out_specs=(P("ctx", "head", None), P(("ctx", "head"), None), P(("ctx", "head"), None)),
        check_vma=False,
    )
```
